32 devices in a mesh: wide: 4 (over y, x), narrow: 8 (over z, core).
Axes of the slice: x: 2, y: 2, z: 4, core: 2. Of those that a mesh axis runs over, the one named last changes fastest.
Arguments:
- model: float32 [64, 2, 256, 256], P(('wide', 'narrow')), may hold values from -6 to 6
- observed: float32 [64, 2, 256, 256], P(('wide', 'narrow')), may hold values from -6 to 6
- own_weights: float32 [5, 64, 2, 256, 256], P(None, ('wide', 'narrow')), may hold values from -0.1875 to 0.1875
- partner_weights: float32 [5, 64, 2, 256, 256], P(None, ('wide', 'narrow')), may hold values from -0.1875 to 0.1875
Outputs:
- residual: float32 [64, 2, 256, 256], P(('wide', 'narrow'))
- gradient: float32 [64, 2, 256, 256], P(('wide', 'narrow'))
The draws below stay inside these ranges and needn't reach their ends.
All inputs are finite; a program needn't handle non-finite values.
Results may differ from the reference program's by a relative error of at most 0.0001.
Values sent between devices are 32-bit elements; how exact they have to be, the bound alone decides.
No kernel may reach another device: no remote copies, remote signals or barrier semaphores. Data moves between devices by JAX's collectives and lax.ppermute only.
A program may use at most 128 MiB of HBM per device.

```python
import jax
import jax.numpy as jnp
from jax import lax

K = 256
LEVELS = 5
ROWS = 256
BOXES = 64
N_WIDE = 4
N_NARROW = 8


def level_of(own_key, extent, pieces, smallest, high):
    level, own = 1.0, jax.random.fold_in(own_key, 6)
    for position, parts in pieces:
        heights = jnp.exp(jax.random.uniform(jax.random.fold_in(own, position), (parts,), jnp.float32, smallest / len(pieces), high / len(pieces)))
        level = level * jnp.repeat(heights, extent[position] // parts).reshape([-1 if axis == position else 1 for axis in range(len(extent))])
    return level


def normal_values(own_key, extent, scale, reach, pieces=(), kind=jnp.bfloat16):
    level = level_of(own_key, extent, pieces, -0.22, 0.18) if pieces else 1.0
    array = jax.random.normal(own_key, extent, jnp.float32) * scale * level
    return jnp.minimum(jnp.maximum(array, -reach), reach).astype(kind)


def setup_inputs(seed: int = 0) -> dict:
    key_of = jax.random.split(jax.random.key(seed), 5)
    return {
        "model": normal_values(key_of[0], (BOXES, 2, ROWS, K), 1.0, 6.0, ((0, 32),), jnp.float32),
        "observed": normal_values(key_of[1], (BOXES, 2, ROWS, K), 1.0, 6.0, ((0, 32),), jnp.float32),
        "own_weights": normal_values(key_of[2], (LEVELS, BOXES, 2, K, K), (4 * K) ** -0.5, 0.1875, ((1, 32),), jnp.float32),
        "partner_weights": normal_values(key_of[3], (LEVELS, BOXES, 2, K, K), (4 * K) ** -0.5, 0.1875, ((1, 32),), jnp.float32),
    }


def mult(u, m):
    def prod(a, b):
        return jnp.einsum('brk,bkm->brm', a, b, precision=lax.Precision.HIGHEST)
    ur, ui = u[:, 0], u[:, 1]
    mr, mi = m[:, 0], m[:, 1]
    return jnp.stack([prod(ur, mr) - prod(ui, mi), prod(ur, mi) + prod(ui, mr)], axis=1)


def mult_adjoint(u, m):
    def prod(a, b):
        return jnp.einsum('brm,bkm->brk', a, b, precision=lax.Precision.HIGHEST)
    ur, ui = u[:, 0], u[:, 1]
    mr, mi = m[:, 0], m[:, 1]
    return jnp.stack([prod(ur, mr) + prod(ui, mi), prod(ui, mr) - prod(ur, mi)], axis=1)


def reference(model, observed, own_weights, partner_weights):
    narrow_bits = N_NARROW.bit_length() - 1
    wide_bits = N_WIDE.bit_length() - 1
    shifts = [0, 1, narrow_bits, 1 + narrow_bits, narrow_bits + wide_bits]
    boxes_index = jnp.arange(model.shape[0], dtype=jnp.int32)
    state = model
    for level in range(LEVELS):
        partner = boxes_index ^ (1 << shifts[level])
        state = mult(state, own_weights[level]) + mult(state[partner], partner_weights[level])
    residual = state - observed
    grad = residual
    for level in reversed(range(LEVELS)):
        partner = boxes_index ^ (1 << shifts[level])
        grad = mult_adjoint(grad, own_weights[level]) + mult_adjoint(grad, partner_weights[level])[partner]
    return residual, grad
```

```python
import functools

import jax
import jax.numpy as jnp
from jax import lax
from jax.experimental import pallas as pl
from jax.experimental.pallas import tpu as pltpu
from jax.sharding import PartitionSpec as P

LEVELS = 5
BF, F32 = jnp.bfloat16, jnp.float32
SHARES = (1, 2, 2, 2, 1)
VMEM = pl.BlockSpec(memory_space=pltpu.VMEM)
HBM = pl.BlockSpec(memory_space=pltpu.HBM)
ANY = pl.BlockSpec(memory_space=pl.ANY)


def split(x):
    high = x.astype(BF)
    return high, (x - high.astype(F32)).astype(BF)


def dot(a, b, transposed):
    return lax.dot_general(a, b, (((1,), (1 if transposed else 0,)), ((), ())), preferred_element_type=F32)


def product(ur, ui, high, low, adjoint):
    rows = ur.shape[0]
    rh, rl = split(ur)
    ih, il = split(ui)
    both = jnp.concatenate([rh, rl, ih, il], 0)
    tops = jnp.concatenate([rh, ih], 0)

    def real(k):
        a, c = dot(both, high[k], adjoint), dot(tops, low[k], adjoint)
        return a[:rows] + a[rows : 2 * rows] + c[:rows], a[2 * rows : 3 * rows] + a[3 * rows :] + c[rows:]

    rr, ir = real(0)
    ri, ii = real(1)
    return (rr + ii, ir - ri) if adjoint else (rr - ii, ri + ir)


def store_adjoint(gr, gi, b, high, low, own, term):
    tr, ti = product(gr, gi, high.at[1, b], low.at[1, b], True)
    term[b, 0], term[b, 1] = tr, ti
    sr, si = product(gr, gi, high.at[0, b], low.at[0, b], True)
    own[b, 0], own[b, 1] = sr, si


def prepare_kernel(level, own, partner, token, high, low, buffer, sems):
    boxes = high.shape[1]
    copies = [
        [pltpu.make_async_copy(source.at[level, b], buffer.at[s, b], sems.at[s, b]) for b in range(boxes)]
        for s, source in enumerate((own, partner))
    ]
    for row in copies:
        for copy in row:
            copy.start()
    for s, row in enumerate(copies):
        for b, copy in enumerate(row):
            copy.wait()
            high[s, b], low[s, b] = split(buffer[s, b])


def first_kernel(start, model, high, low, token, out):
    boxes, rows = out.shape[0], out.shape[2]
    at = pl.ds(start, rows)
    for b in range(boxes):
        r0, i0 = product(model[b, 0, at], model[b, 1, at], high.at[0, b], low.at[0, b], False)
        r1, i1 = product(model[b ^ 1, 0, at], model[b ^ 1, 1, at], high.at[1, b], low.at[1, b], False)
        out[b, 0], out[b, 1] = r0 + r1, i0 + i1


def forward_kernel(state, other, high, low, token, out):
    for b in range(out.shape[0]):
        r0, i0 = product(state[b, 0], state[b, 1], high.at[0, b], low.at[0, b], False)
        r1, i1 = product(other[b, 0], other[b, 1], high.at[1, b], low.at[1, b], False)
        out[b, 0], out[b, 1] = r0 + r1, i0 + i1


def turn_kernel(start, aliased, state, other, high, low, observed, token, *refs):
    own, term, residual, buffer, sem = refs[1:] if aliased else refs
    rows = state.shape[2]
    at = pl.ds(start, rows)
    copy = pltpu.make_async_copy(buffer, residual.at[:, :, at], sem)
    for b in range(state.shape[0]):
        r0, i0 = product(state[b, 0], state[b, 1], high.at[0, b], low.at[0, b], False)
        r1, i1 = product(other[b, 0], other[b, 1], high.at[1, b], low.at[1, b], False)
        buffer[b, 0] = r0 + r1 - observed[b, 0, at]
        buffer[b, 1] = i0 + i1 - observed[b, 1, at]
    copy.start()
    for b in range(state.shape[0]):
        store_adjoint(buffer[b, 0], buffer[b, 1], b, high, low, own, term)
    copy.wait()


def backward_kernel(grad, carried, high, low, token, own, term):
    for b in range(grad.shape[0]):
        store_adjoint(grad[b, 0] + carried[b, 0], grad[b, 1] + carried[b, 1], b, high, low, own, term)


def last_kernel(start, aliased, grad, carried, high, low, token, *refs):
    done, out, buffer, sem = refs[1:] if aliased else refs
    boxes, rows = grad.shape[0], grad.shape[2]
    copy = pltpu.make_async_copy(buffer, out.at[:, :, pl.ds(start, rows)], sem)
    g = [(grad[b, 0] + carried[b, 0], grad[b, 1] + carried[b, 1]) for b in range(boxes)]
    for b in range(boxes):
        r0, i0 = product(*g[b], high.at[0, b], low.at[0, b], True)
        r1, i1 = product(*g[b ^ 1], high.at[1, b ^ 1], low.at[1, b ^ 1], True)
        buffer[b, 0], buffer[b, 1] = r0 + r1, i0 + i1
    copy.start()
    done[...] = jnp.zeros_like(done)
    copy.wait()


def call(name, kernel, operands, specs, outs, out_specs, scratch=(), aliases=None):
    return pl.pallas_call(
        kernel,
        out_shape=outs,
        in_specs=specs,
        out_specs=out_specs,
        scratch_shapes=scratch,
        input_output_aliases=aliases or {},
        compiler_params=pltpu.CompilerParams(vmem_limit_bytes=10 << 20),
        name=name,
    )(*operands)


def schedule(chunks, rows, link_us):
    crossing = {0: 1, 1: 2, 2: 3, 3: 4, 4: 4, 5: 3, 6: 2, 7: 1}
    ready = {(0, c): 0.0 for c in range(len(chunks))}
    free = {level: 0.0 for level in range(LEVELS)}
    now, order = 2.0, []
    while ready:
        def key(item):
            (stage, c), at = item
            return (max(at, now), c, -stage)
        (stage, c), at = min(ready.items(), key=key)
        del ready[stage, c]
        now = max(now, at) + 0.4 + 0.6 * chunks[c] / (rows / 4) * (2.0 if stage == 4 else 1.0)
        order.append((stage, c))
        if stage < 8:
            level = crossing[stage]
            begin = max(now, free[level])
            free[level] = begin + link_us[level] * chunks[c] / rows
            ready[stage + 1, c] = free[level] + 1.5
    return order


def shards(model, observed, own_weights, partner_weights):
    narrow, wide = lax.axis_size("narrow"), lax.axis_size("wide")
    exchanges = {
        1: ("narrow", 1, 4.0),
        2: ("narrow", narrow // 2, 46.0),
        3: ("wide", 1, 23.0),
        4: ("wide", wide // 2, 23.0),
    }
    boxes, parts, rows, k = model.shape
    unit = rows // sum(SHARES)
    chunks = [share * unit for share in SHARES]
    starts = [sum(chunks[:c]) for c in range(len(chunks))]
    order = schedule(chunks, rows, {level: us for level, (_, _, us) in exchanges.items()})

    def swap(value, level):
        axis, mask, _ = exchanges[level]
        return lax.ppermute(value, axis, [(i, i ^ mask) for i in range(lax.axis_size(axis))])

    def in_vmem(x):
        return pltpu.with_memory_space_constraint(x, pltpu.VMEM)

    weights, state, other = {}, {}, {}
    held = (in_vmem(model), in_vmem(observed))
    token = held[0]
    residual = gradient = None

    def prepare(level, token):
        shape = pltpu.VMEM((2,) + own_weights.shape[1:], BF)
        return call(
            f"prepare{level}",
            functools.partial(prepare_kernel, level),
            (own_weights, partner_weights, token),
            [HBM, HBM, ANY],
            (shape, shape),
            (VMEM, VMEM),
            [pltpu.VMEM((2,) + own_weights.shape[1:], F32), pltpu.SemaphoreType.DMA((2, boxes))],
        )

    for stage, c in order:
        level = stage if stage < LEVELS else 2 * LEVELS - 2 - stage
        if level not in weights:
            weights[level] = prepare(level, token)
            token = weights[level][0]
        high, low = weights[level]
        chunk = pltpu.VMEM((boxes, parts, chunks[c], k), F32)
        whole = pltpu.HBM(model.shape, F32)
        bounce = [pltpu.VMEM((boxes, parts, chunks[c], k), F32), pltpu.SemaphoreType.DMA]
        name = f"stage{stage}_{c}"
        if stage == 0:
            state[c] = call(name, functools.partial(first_kernel, starts[c]), (held[0], high, low, token), [VMEM] * 3 + [ANY], chunk, VMEM)
            token = state[c]
            other[c] = swap(state[c], 1)
        elif stage < LEVELS - 1:
            state[c] = call(name, forward_kernel, (state[c], other[c], high, low, token), [VMEM] * 4 + [ANY], chunk, VMEM)
            token = state[c]
            other[c] = swap(state[c], level + 1)
        elif stage == LEVELS - 1:
            more = () if residual is None else (residual,)
            state[c], term, residual = call(
                name,
                functools.partial(turn_kernel, starts[c], bool(more)),
                (state[c], other[c], high, low, held[1], token, *more),
                [VMEM] * 5 + [ANY] + [HBM] * len(more),
                (chunk, chunk, whole),
                (VMEM, VMEM, HBM),
                bounce,
                {6: 2} if more else None,
            )
            token = state[c]
            other[c] = swap(term, level)
        elif level > 0:
            state[c], term = call(name, backward_kernel, (state[c], other[c], high, low, token), [VMEM] * 4 + [ANY], (chunk, chunk), (VMEM, VMEM))
            token = state[c]
            other[c] = swap(term, level)
        else:
            more = () if gradient is None else (gradient,)
            token, gradient = call(
                name,
                functools.partial(last_kernel, starts[c], bool(more)),
                (state[c], other[c], high, low, token, *more),
                [VMEM] * 4 + [ANY] + [HBM] * len(more),
                (pltpu.VMEM((8, 128), F32), whole),
                (VMEM, HBM),
                bounce,
                {5: 1} if more else None,
            )
    return residual, gradient


def solution(mesh):
    boxes = P(("wide", "narrow"), None, None, None)
    matrices = P(None, ("wide", "narrow"), None, None, None)
    return jax.shard_map(
        shards, mesh=mesh, in_specs=(boxes, boxes, matrices, matrices), out_specs=(boxes, boxes), check_vma=False
    )
```

```python
import functools

import jax
import jax.numpy as jnp
from jax import lax
from jax.experimental import pallas as pl
from jax.experimental.pallas import tpu as pltpu
from jax.sharding import PartitionSpec as P


LEVELS = 5
BF, F32 = jnp.bfloat16, jnp.float32
SHARES = (1, 2, 2, 2, 1)
VMEM = pl.BlockSpec(memory_space=pltpu.VMEM)
HBM = pl.BlockSpec(memory_space=pltpu.HBM)
ANY = pl.BlockSpec(memory_space=pl.ANY)


def split(x):
    high = x.astype(BF)
    return high, (x - high.astype(F32)).astype(BF)


def dot(a, b, transposed):
    return lax.dot_general(a, b, (((1,), (1 if transposed else 0,)), ((), ())), preferred_element_type=F32)


def product(ur, ui, high, low, adjoint):
    rows = ur.shape[0]
    rh, rl = split(ur)
    ih, il = split(ui)
    both = jnp.concatenate([rh, rl, ih, il], 0)
    tops = jnp.concatenate([rh, ih], 0)

    def real(k):
        a, c = dot(both, high[k], adjoint), dot(tops, low[k], adjoint)
        return a[:rows] + a[rows : 2 * rows] + c[:rows], a[2 * rows : 3 * rows] + a[3 * rows :] + c[rows:]

    rr, ir = real(0)
    ri, ii = real(1)
    return (rr + ii, ir - ri) if adjoint else (rr - ii, ri + ir)


def store_adjoint(gr, gi, b, high, low, own, term):
    tr, ti = product(gr, gi, high.at[1, b], low.at[1, b], True)
    term[b, 0], term[b, 1] = tr, ti
    sr, si = product(gr, gi, high.at[0, b], low.at[0, b], True)
    own[b, 0], own[b, 1] = sr, si


def prepare_kernel(level, own, partner, *refs):
    high, low, buffer, sems = refs[-4:]
    boxes = high.shape[1]
    copies = [
        [pltpu.make_async_copy(source.at[level, b], buffer.at[s, b], sems.at[s, b]) for b in range(boxes)]
        for s, source in enumerate((own, partner))
    ]
    for row in copies:
        for copy in row:
            copy.start()
    for s, row in enumerate(copies):
        for b, copy in enumerate(row):
            copy.wait()
            high[s, b], low[s, b] = split(buffer[s, b])


def first_kernel(start, model, high, low, token, out):
    boxes, rows = out.shape[0], out.shape[2]
    at = pl.ds(start, rows)
    for b in range(boxes):
        r0, i0 = product(model[b, 0, at], model[b, 1, at], high.at[0, b], low.at[0, b], False)
        r1, i1 = product(model[b ^ 1, 0, at], model[b ^ 1, 1, at], high.at[1, b], low.at[1, b], False)
        out[b, 0], out[b, 1] = r0 + r1, i0 + i1


def forward_kernel(state, other, high, low, token, out):
    for b in range(out.shape[0]):
        r0, i0 = product(state[b, 0], state[b, 1], high.at[0, b], low.at[0, b], False)
        r1, i1 = product(other[b, 0], other[b, 1], high.at[1, b], low.at[1, b], False)
        out[b, 0], out[b, 1] = r0 + r1, i0 + i1


def turn_kernel(start, aliased, state, other, high, low, observed, token, *refs):
    own, term, residual, buffer, sem = refs[1:] if aliased else refs
    rows = state.shape[2]
    at = pl.ds(start, rows)
    copy = pltpu.make_async_copy(buffer, residual.at[:, :, at], sem)
    for b in range(state.shape[0]):
        r0, i0 = product(state[b, 0], state[b, 1], high.at[0, b], low.at[0, b], False)
        r1, i1 = product(other[b, 0], other[b, 1], high.at[1, b], low.at[1, b], False)
        buffer[b, 0] = r0 + r1 - observed[b, 0, at]
        buffer[b, 1] = i0 + i1 - observed[b, 1, at]
    copy.start()
    for b in range(state.shape[0]):
        store_adjoint(buffer[b, 0], buffer[b, 1], b, high, low, own, term)
    copy.wait()


def backward_kernel(grad, carried, high, low, token, own, term):
    for b in range(grad.shape[0]):
        store_adjoint(grad[b, 0] + carried[b, 0], grad[b, 1] + carried[b, 1], b, high, low, own, term)


def last_kernel(start, aliased, grad, carried, high, low, token, *refs):
    done, out, buffer, sem = refs[1:] if aliased else refs
    boxes, rows = grad.shape[0], grad.shape[2]
    copy = pltpu.make_async_copy(buffer, out.at[:, :, pl.ds(start, rows)], sem)
    g = [(grad[b, 0] + carried[b, 0], grad[b, 1] + carried[b, 1]) for b in range(boxes)]
    for b in range(boxes):
        r0, i0 = product(*g[b], high.at[0, b], low.at[0, b], True)
        r1, i1 = product(*g[b ^ 1], high.at[1, b ^ 1], low.at[1, b ^ 1], True)
        buffer[b, 0], buffer[b, 1] = r0 + r1, i0 + i1
    copy.start()
    done[...] = jnp.zeros_like(done)
    copy.wait()


def call(kernel, operands, specs, outs, out_specs, scratch=(), aliases=None):
    return pl.pallas_call(
        kernel,
        out_shape=outs,
        in_specs=specs,
        out_specs=out_specs,
        scratch_shapes=scratch,
        input_output_aliases=aliases or {},
        compiler_params=pltpu.CompilerParams(vmem_limit_bytes=10 << 20),
    )(*operands)


def schedule(chunks, rows, link_us):
    crossing = {0: 1, 1: 2, 2: 3, 3: 4, 4: 4, 5: 3, 6: 2, 7: 1}
    ready = {(0, c): 0.0 for c in range(len(chunks))}
    free = {level: 0.0 for level in range(LEVELS)}
    now, order = 2.0, []
    while ready:
        def key(item):
            (stage, c), at = item
            return (max(at, now), c, -stage)

        (stage, c), at = min(ready.items(), key=key)
        del ready[stage, c]
        now = max(now, at) + 0.4 + 0.6 * chunks[c] / (rows / 4) * (2.0 if stage == 4 else 1.0)
        order.append((stage, c))
        if stage < 8:
            level = crossing[stage]
            begin = max(now, free[level])
            free[level] = begin + link_us[level] * chunks[c] / rows
            ready[stage + 1, c] = free[level] + 1.5
    return order


LINK_US = {1: 4.0, 2: 46.0, 3: 23.0, 4: 23.0}


def shards(order, model, observed, own_weights, partner_weights):
    narrow, wide = lax.axis_size("narrow"), lax.axis_size("wide")
    exchanges = {1: ("narrow", 1), 2: ("narrow", narrow // 2), 3: ("wide", 1), 4: ("wide", wide // 2)}
    boxes, parts, rows, k = model.shape
    unit = rows // sum(SHARES)
    chunks = [share * unit for share in SHARES]
    starts = [sum(chunks[:c]) for c in range(len(chunks))]

    def swap(value, level):
        axis, mask = exchanges[level]
        return lax.ppermute(value, axis, [(i, i ^ mask) for i in range(lax.axis_size(axis))])

    def in_vmem(x):
        return pltpu.with_memory_space_constraint(x, pltpu.VMEM)

    weights, state, other = {}, {}, {}
    held = (in_vmem(model), in_vmem(observed))
    stored = tuple(pltpu.with_memory_space_constraint(x, pltpu.HBM) for x in (own_weights, partner_weights))
    token = None
    residual = gradient = None

    def prepare(level, token):
        shape = pltpu.VMEM((2,) + own_weights.shape[1:], BF)
        tokens = () if token is None else (token,)
        return call(
            functools.partial(prepare_kernel, level),
            (*stored, *tokens),
            [HBM, HBM] + [ANY] * len(tokens),
            (shape, shape),
            (VMEM, VMEM),
            [pltpu.VMEM((2,) + own_weights.shape[1:], F32), pltpu.SemaphoreType.DMA((2, boxes))],
        )

    for stage, c in order:
        level = stage if stage < LEVELS else 2 * LEVELS - 2 - stage
        if level not in weights:
            weights[level] = prepare(level, token)
            token = weights[level][0]
        high, low = weights[level]
        chunk = pltpu.VMEM((boxes, parts, chunks[c], k), F32)
        whole = pltpu.HBM(model.shape, F32)
        bounce = [pltpu.VMEM((boxes, parts, chunks[c], k), F32), pltpu.SemaphoreType.DMA]
        if stage == 0:
            state[c] = call(functools.partial(first_kernel, starts[c]), (held[0], high, low, token), [VMEM] * 3 + [ANY], chunk, VMEM)
            token = state[c]
            other[c] = swap(state[c], 1)
        elif stage < LEVELS - 1:
            state[c] = call(forward_kernel, (state[c], other[c], high, low, token), [VMEM] * 4 + [ANY], chunk, VMEM)
            token = state[c]
            other[c] = swap(state[c], level + 1)
        elif stage == LEVELS - 1:
            more = () if residual is None else (residual,)
            state[c], term, residual = call(
                functools.partial(turn_kernel, starts[c], bool(more)),
                (state[c], other[c], high, low, held[1], token, *more),
                [VMEM] * 5 + [ANY] + [HBM] * len(more),
                (chunk, chunk, whole),
                (VMEM, VMEM, HBM),
                bounce,
                {6: 2} if more else None,
            )
            token = state[c]
            other[c] = swap(term, level)
        elif level > 0:
            state[c], term = call(backward_kernel, (state[c], other[c], high, low, token), [VMEM] * 4 + [ANY], (chunk, chunk), (VMEM, VMEM))
            token = state[c]
            other[c] = swap(term, level)
        else:
            more = () if gradient is None else (gradient,)
            token, gradient = call(
                functools.partial(last_kernel, starts[c], bool(more)),
                (state[c], other[c], high, low, token, *more),
                [VMEM] * 4 + [ANY] + [HBM] * len(more),
                (pltpu.VMEM((8, 128), F32), whole),
                (VMEM, HBM),
                bounce,
                {5: 1} if more else None,
            )
    return residual, gradient


def solution(mesh):
    boxes = P(("wide", "narrow"), None, None, None)
    matrices = P(None, ("wide", "narrow"), None, None, None)
    order = schedule(SHARES, sum(SHARES), LINK_US)

    def step(*arrays):
        return shards(order, *arrays)

    return jax.shard_map(
        step, mesh=mesh, in_specs=(boxes, boxes, matrices, matrices), out_specs=(boxes, boxes), check_vma=False
    )
```

```python
import functools
from typing import NamedTuple

import jax
import jax.numpy as jnp
from jax import lax
from jax.experimental import pallas as pl
from jax.experimental.pallas import tpu as pltpu
from jax.sharding import PartitionSpec as P


LEVELS = 5
BF, F32 = jnp.bfloat16, jnp.float32
SHARES = (2, 3, 3, 3, 3, 2)
ORDER = (((9, 0),), ((0, 0),), ((9, 1),), ((1, 0),), ((9, 2),), ((0, 1),), ((0, 3),), ((0, 2),), ((1, 1),), ((0, 4),), ((1, 2),), ((0, 5),), ((2, 0),), ((9, 3),), ((3, 0),), ((9, 4),), ((2, 1),), ((1, 3),), ((4, 0),), ((2, 2),), ((3, 1),), ((1, 4),), ((3, 2),), ((2, 3),), ((4, 1),), ((5, 0),), ((4, 2),), ((1, 5),), ((2, 4), (5, 1)), ((6, 0),), ((3, 3),), ((5, 2),), ((2, 5),), ((3, 4),), ((6, 1),), ((4, 3),), ((6, 2),), ((4, 4),), ((5, 3),), ((3, 5),), ((5, 4),), ((6, 3),), ((4, 5),), ((7, 0),), ((6, 4),), ((7, 2),), ((7, 1),), ((5, 5),), ((8, 0),), ((8, 1),), ((8, 2),), ((6, 5),), ((7, 3),), ((7, 4),), ((8, 3), (8, 4)), ((7, 5),), ((8, 5),))
VMEM = pl.BlockSpec(memory_space=pltpu.VMEM)
HBM = pl.BlockSpec(memory_space=pltpu.HBM)
ANY = pl.BlockSpec(memory_space=pl.ANY)


def split(x):
    high = x.astype(BF)
    return high, (x - high.astype(F32)).astype(BF)


def dot(a, b, transposed):
    return lax.dot_general(a, b, (((1,), (1 if transposed else 0,)), ((), ())), preferred_element_type=F32)


def product(ur, ui, high, low, adjoint):
    rows = ur.shape[0]
    rh, rl = split(ur)
    ih, il = split(ui)
    both = jnp.concatenate([rh, rl, ih, il], 0)
    tops = jnp.concatenate([rh, ih], 0)

    def real(k):
        a, c = dot(both, high[k], adjoint), dot(tops, low[k], adjoint)
        return a[:rows] + a[rows : 2 * rows] + c[:rows], a[2 * rows : 3 * rows] + a[3 * rows :] + c[rows:]

    rr, ir = real(0)
    ri, ii = real(1)
    return (rr + ii, ir - ri) if adjoint else (rr - ii, ri + ir)


def prepare_kernel(level, own, partner, *refs):
    high, low, buffer, sems = refs[-4:]
    boxes = high.shape[1]
    copies = [
        [pltpu.make_async_copy(source.at[level, b], buffer.at[s, b], sems.at[s, b]) for b in range(boxes)]
        for s, source in enumerate((own, partner))
    ]
    for row in copies:
        for copy in row:
            copy.start()
    for s, row in enumerate(copies):
        for b, copy in enumerate(row):
            copy.wait()
            high[s, b], low[s, b] = split(buffer[s, b])


class Task(NamedTuple):
    stage: int
    rows: int
    ours: tuple
    theirs: tuple
    weights: int
    sent: tuple = ()
    kept: int = -1
    observed: int = -1
    result: tuple = ()


def group_kernel(tasks, *refs):
    copies = []
    for task in tasks:
        (ours, start), (theirs, other) = ((refs[ref], pl.ds(row, task.rows)) for ref, row in (task.ours, task.theirs))
        high, low = refs[task.weights], refs[task.weights + 1]
        boxes = range(ours.shape[0])
        if task.sent:
            out, at = refs[task.sent[0]], pl.ds(task.sent[1], task.rows)
        if task.result:
            whole, row, buffer, sems = task.result
            buffer, final = refs[buffer], pl.ds(row, task.rows)
            writes = [
                pltpu.make_async_copy(buffer.at[b], refs[whole].at[b, :, final], refs[sems].at[b]) for b in boxes
            ]
            copies += writes
        if task.stage < LEVELS:
            for b in boxes:
                p = b ^ 1 if task.stage == 0 else b
                r0, i0 = product(ours[b, 0, start], ours[b, 1, start], high.at[0, b], low.at[0, b], False)
                r1, i1 = product(theirs[p, 0, other], theirs[p, 1, other], high.at[1, b], low.at[1, b], False)
                if task.stage < LEVELS - 1:
                    out[b, 0, at], out[b, 1, at] = r0 + r1, i0 + i1
                else:
                    observed = refs[task.observed]
                    buffer[b, 0] = r0 + r1 - observed[b, 0, final]
                    buffer[b, 1] = i0 + i1 - observed[b, 1, final]
                    writes[b].start()
            if task.stage < LEVELS - 1:
                continue
            grads = [(buffer[b, 0], buffer[b, 1]) for b in boxes]
        else:
            grads = [
                (ours[b, 0, start] + theirs[b, 0, other], ours[b, 1, start] + theirs[b, 1, other]) for b in boxes
            ]
        for b in boxes:
            if task.sent:
                out[b, 0, at], out[b, 1, at] = product(*grads[b], high.at[1, b], low.at[1, b], True)
            sr, si = product(*grads[b], high.at[0, b], low.at[0, b], True)
            if task.sent:
                kept = refs[task.kept]
                kept[b, 0], kept[b, 1] = sr, si
            else:
                p = b ^ 1
                tr, ti = product(*grads[p], high.at[1, p], low.at[1, p], True)
                buffer[b, 0], buffer[b, 1] = sr + tr, si + ti
                writes[b].start()
    for copy in copies:
        copy.wait()


def call(kernel, operands, specs, outs, out_specs, scratch=(), aliases=None):
    return pl.pallas_call(
        kernel,
        out_shape=outs,
        in_specs=specs,
        out_specs=out_specs,
        scratch_shapes=scratch,
        input_output_aliases=aliases or {},
        compiler_params=pltpu.CompilerParams(vmem_limit_bytes=10 << 20),
    )(*operands)


def shards(model, observed, own_weights, partner_weights):
    narrow, wide = lax.axis_size("narrow"), lax.axis_size("wide")
    exchanges = {1: ("narrow", 1), 2: ("narrow", narrow // 2), 3: ("wide", 1), 4: ("wide", wide // 2)}
    boxes, parts, rows, k = model.shape
    edges = [sum(SHARES[:c]) * rows // sum(SHARES) for c in range(len(SHARES) + 1)]

    def swap(value, level):
        axis, mask = exchanges[level]
        return lax.ppermute(value, axis, [(i, i ^ mask) for i in range(lax.axis_size(axis))])

    def rows_of(count):
        return pltpu.VMEM((boxes, parts, count, k), F32)

    model, observed = (pltpu.with_memory_space_constraint(x, pltpu.VMEM) for x in (model, observed))
    stored = [pltpu.with_memory_space_constraint(x, pltpu.HBM) for x in (own_weights, partner_weights)]
    matrices = (2,) + own_weights.shape[1:]
    weights = {}
    ours = {c: (model, edges[c]) for c in range(len(SHARES))}
    theirs = dict(ours)
    results = {}
    token = None

    for group in ORDER:
        stage, c = group[0]
        if stage == 9:
            tokens = [] if token is None else [token]
            weights[c] = call(
                functools.partial(prepare_kernel, c),
                stored + tokens,
                [HBM, HBM] + [ANY] * len(tokens),
                (pltpu.VMEM(matrices, BF),) * 2,
                (VMEM, VMEM),
                [pltpu.VMEM(matrices, F32), pltpu.SemaphoreType.DMA((2, boxes))],
            )
            token = weights[c][0]
            continue
        operands, specs, outs, out_specs, scratch, aliases, plans = [], [], [], [], [], {}, []

        def operand(array, spec=VMEM):
            for at, known in enumerate(operands):
                if known is array:
                    return at
            operands.append(array)
            specs.append(spec)
            return len(operands) - 1

        counts = [edges[c + 1] - edges[c] for _, c in group]
        sends = exchange_of(stage)
        if sends:
            outs.append(rows_of(sum(counts)))
            out_specs.append(VMEM)
        else:
            outs.append(pltpu.VMEM((8, 128), F32))
            out_specs.append(VMEM)
        row, places = 0, {}
        for (stage, c), count in zip(group, counts):
            level = level_of(stage)
            plan = {
                "stage": stage,
                "rows": count,
                "ours": (operand(ours[c][0]), ours[c][1]),
                "theirs": (operand(theirs[c][0]), theirs[c][1]),
            }
            pair = [x for x in weights[level]]
            plan["weights"] = next((at for at, known in enumerate(operands) if known is pair[0]), len(operands))
            for x in pair:
                operand(x)
            if sends:
                plan["sent"] = (0, row)
            if LEVELS - 1 <= stage < 8:
                plan["kept"] = len(outs)
                outs.append(rows_of(count))
                out_specs.append(VMEM)
            if stage == LEVELS - 1:
                plan["observed"] = operand(observed)
            if stage in (LEVELS - 1, 8):
                if stage not in places:
                    if stage in results:
                        aliases[operand(results[stage], HBM)] = len(outs)
                    places[stage] = len(outs)
                    outs.append(pltpu.HBM((boxes, parts, rows, k), F32))
                    out_specs.append(HBM)
                plan["result"] = (places[stage], edges[c], len(scratch), len(scratch) + 1)
                scratch += [rows_of(count), pltpu.SemaphoreType.DMA((boxes,))]
            plans.append(plan)
            row += count
        operand(token, ANY)
        first, second = len(operands), len(operands) + len(outs)
        for plan in plans:
            if "sent" in plan:
                plan["sent"] = (first + plan["sent"][0], plan["sent"][1])
            if "kept" in plan:
                plan["kept"] += first
            if "result" in plan:
                whole, at, buffer, sems = plan["result"]
                plan["result"] = (first + whole, at, second + buffer, second + sems)
        tasks = tuple(Task(**plan) for plan in plans)
        made = call(functools.partial(group_kernel, tasks), operands, specs, outs, out_specs, scratch, aliases)
        token = made[0]
        for stage, at in places.items():
            results[stage] = made[at]
        if not sends:
            continue
        received = swap(token, sends)
        for task, (stage, c) in zip(tasks, group):
            at = task.sent[1]
            ours[c] = (token, at) if task.kept < 0 else (made[task.kept - first], 0)
            theirs[c] = (received, at)
    return results[LEVELS - 1], results[8]


def level_of(stage):
    return stage if stage < LEVELS else 2 * LEVELS - 2 - stage


def exchange_of(stage):
    return stage + 1 if stage < LEVELS - 1 else level_of(stage)


def solution(mesh):
    boxes = P(("wide", "narrow"), None, None, None)
    matrices = P(None, ("wide", "narrow"), None, None, None)

    return jax.shard_map(
        shards, mesh=mesh, in_specs=(boxes, boxes, matrices, matrices), out_specs=(boxes, boxes), check_vma=False
    )
```

```python
import functools
from typing import NamedTuple

import jax
import jax.numpy as jnp
from jax import lax
from jax.experimental import pallas as pl
from jax.experimental.pallas import tpu as pltpu
from jax.sharding import PartitionSpec as P


LEVELS = 5
BF, F32 = jnp.bfloat16, jnp.float32
SHARES = (3, 3, 4, 3, 3)
ORDER = (((9, 0),), ((0, 0),), ((9, 1),), ((1, 0),), ((0, 2),), ((9, 4),), ((0, 1),), ((9, 3),), ((1, 2),), ((9, 2),), ((2, 0),), ((0, 3),), ((1, 1),), ((3, 0),), ((2, 2),), ((0, 4),), ((10, 1),), ((4, 0),), ((1, 3),), ((3, 2),), ((2, 1),), ((1, 4),), ((5, 0),), ((4, 2),), ((2, 3),), ((3, 1),), ((10, 0),), ((6, 0),), ((5, 2),), ((3, 3),), ((2, 4),), ((4, 1),), ((6, 2),), ((4, 3),), ((5, 1),), ((3, 4),), ((5, 3),), ((6, 1),), ((7, 0),), ((4, 4),), ((6, 3),), ((5, 4),), ((8, 0),), ((7, 1),), ((7, 2),), ((8, 1),), ((6, 4),), ((8, 2),), ((7, 3),), ((8, 3),), ((7, 4),), ((8, 4),))
VMEM = pl.BlockSpec(memory_space=pltpu.VMEM)
HBM = pl.BlockSpec(memory_space=pltpu.HBM)
ANY = pl.BlockSpec(memory_space=pl.ANY)


def split(x):
    high = x.astype(BF)
    return high, (x - high.astype(F32)).astype(BF)


def dot(a, b):
    return lax.dot_general(a, b, (((1,), (0,)), ((), ())), preferred_element_type=F32)


def product(ur, ui, high, low, adjoint):
    rows = ur.shape[0]
    rh, rl = split(ur)
    ih, il = split(ui)
    both = jnp.concatenate([rh, rl, ih, il], 0)
    tops = jnp.concatenate([rh, ih], 0)

    def real(k):
        a, c = dot(both, high[k]), dot(tops, low[k])
        return a[:rows] + a[rows : 2 * rows] + c[:rows], a[2 * rows : 3 * rows] + a[3 * rows :] + c[rows:]

    rr, ir = real(0)
    ri, ii = real(1)
    return (rr + ii, ir - ri) if adjoint else (rr - ii, ri + ir)


def store_transposes(s, b, high, low, flipped):
    for k in range(high.shape[2]):
        flipped[0][s, b, k] = high[s, b, k].T
        flipped[1][s, b, k] = low[s, b, k].T


def prepare_kernel(level, count, own, partner, *refs):
    high, low, *flipped = refs[-2 - count : -2]
    buffer, sems = refs[-2:]
    boxes = high.shape[1]
    copies = [
        [pltpu.make_async_copy(source.at[level, b], buffer.at[s, b], sems.at[s, b]) for b in range(boxes)]
        for s, source in enumerate((own, partner))
    ]
    for row in copies:
        for copy in row:
            copy.start()
    for s, row in enumerate(copies):
        for b, copy in enumerate(row):
            copy.wait()
            high[s, b], low[s, b] = split(buffer[s, b])
            if flipped:
                store_transposes(s, b, high, low, flipped)


def flip_kernel(high, low, token, *flipped):
    for s in range(high.shape[0]):
        for b in range(high.shape[1]):
            store_transposes(s, b, high, low, flipped)


class Task(NamedTuple):
    stage: int
    rows: int
    ours: tuple
    theirs: tuple
    weights: int
    flipped: int = -1
    sent: tuple = ()
    kept: int = -1
    observed: int = -1
    result: tuple = ()


def group_kernel(tasks, *refs):
    copies = []
    for task in tasks:
        (ours, start), (theirs, other) = ((refs[ref], pl.ds(row, task.rows)) for ref, row in (task.ours, task.theirs))
        high, low = refs[task.weights], refs[task.weights + 1]
        boxes = range(ours.shape[0])
        if task.sent:
            out, at = refs[task.sent[0]], pl.ds(task.sent[1], task.rows)
        if task.result:
            whole, row, buffer, sems = task.result
            buffer, final = refs[buffer], pl.ds(row, task.rows)
            writes = [
                pltpu.make_async_copy(buffer.at[b], refs[whole].at[b, :, final], refs[sems].at[b]) for b in boxes
            ]
            copies += writes
        if task.stage < LEVELS:
            for b in boxes:
                p = b ^ 1 if task.stage == 0 else b
                r0, i0 = product(ours[b, 0, start], ours[b, 1, start], high.at[0, b], low.at[0, b], False)
                r1, i1 = product(theirs[p, 0, other], theirs[p, 1, other], high.at[1, b], low.at[1, b], False)
                if task.stage < LEVELS - 1:
                    out[b, 0, at], out[b, 1, at] = r0 + r1, i0 + i1
                else:
                    observed = refs[task.observed]
                    buffer[b, 0] = r0 + r1 - observed[b, 0, final]
                    buffer[b, 1] = i0 + i1 - observed[b, 1, final]
                    writes[b].start()
            if task.stage < LEVELS - 1:
                continue
            grads = [(buffer[b, 0], buffer[b, 1]) for b in boxes]
            high, low = refs[task.flipped], refs[task.flipped + 1]
        else:
            grads = [
                (ours[b, 0, start] + theirs[b, 0, other], ours[b, 1, start] + theirs[b, 1, other]) for b in boxes
            ]
        for b in boxes:
            if task.sent:
                out[b, 0, at], out[b, 1, at] = product(*grads[b], high.at[1, b], low.at[1, b], True)
            sr, si = product(*grads[b], high.at[0, b], low.at[0, b], True)
            if task.sent:
                kept = refs[task.kept]
                kept[b, 0], kept[b, 1] = sr, si
            else:
                p = b ^ 1
                tr, ti = product(*grads[p], high.at[1, p], low.at[1, p], True)
                buffer[b, 0], buffer[b, 1] = sr + tr, si + ti
                writes[b].start()
    for copy in copies:
        copy.wait()


def call(kernel, operands, specs, outs, out_specs, scratch=(), aliases=None):
    return pl.pallas_call(
        kernel,
        out_shape=outs,
        in_specs=specs,
        out_specs=out_specs,
        scratch_shapes=scratch,
        input_output_aliases=aliases or {},
        compiler_params=pltpu.CompilerParams(vmem_limit_bytes=10 << 20),
    )(*operands)


def shards(model, observed, own_weights, partner_weights):
    narrow, wide = lax.axis_size("narrow"), lax.axis_size("wide")
    exchanges = {1: ("narrow", 1), 2: ("narrow", narrow // 2), 3: ("wide", 1), 4: ("wide", wide // 2)}
    boxes, parts, rows, k = model.shape
    edges = [sum(SHARES[:c]) * rows // sum(SHARES) for c in range(len(SHARES) + 1)]

    def swap(value, level):
        axis, mask = exchanges[level]
        return lax.ppermute(value, axis, [(i, i ^ mask) for i in range(lax.axis_size(axis))])

    def rows_of(count):
        return pltpu.VMEM((boxes, parts, count, k), F32)

    model, observed = (pltpu.with_memory_space_constraint(x, pltpu.VMEM) for x in (model, observed))
    stored = [pltpu.with_memory_space_constraint(x, pltpu.HBM) for x in (own_weights, partner_weights)]
    matrices = (2,) + own_weights.shape[1:]
    weights, flipped = {}, {}
    later = {c for group in ORDER for stage, c in group if stage == 10}
    ours = {c: (model, edges[c]) for c in range(len(SHARES))}
    theirs = dict(ours)
    results = {}
    token = None

    for group in ORDER:
        stage, c = group[0]
        if stage == 9:
            tokens = [] if token is None else [token]
            count = 2 if c in later else 4
            made = call(
                functools.partial(prepare_kernel, c, count),
                stored + tokens,
                [HBM, HBM] + [ANY] * len(tokens),
                (pltpu.VMEM(matrices, BF),) * count,
                (VMEM,) * count,
                [pltpu.VMEM(matrices, F32), pltpu.SemaphoreType.DMA((2, boxes))],
            )
            weights[c], flipped[c] = made[:2], made[2:]
            token = made[0]
            continue
        if stage == 10:
            flipped[c] = call(
                flip_kernel, [*weights[c], token], [VMEM, VMEM, ANY], (pltpu.VMEM(matrices, BF),) * 2, (VMEM,) * 2
            )
            token = flipped[c][0]
            continue
        operands, specs, outs, out_specs, scratch, aliases, plans = [], [], [], [], [], {}, []

        def operand(array, spec=VMEM):
            for at, known in enumerate(operands):
                if known is array:
                    return at
            operands.append(array)
            specs.append(spec)
            return len(operands) - 1

        def pair_of(matrices):
            at = operand(matrices[0])
            operand(matrices[1])
            return at

        counts = [edges[c + 1] - edges[c] for _, c in group]
        sends = exchange_of(stage)
        if sends:
            outs.append(rows_of(sum(counts)))
            out_specs.append(VMEM)
        else:
            outs.append(pltpu.VMEM((8, 128), F32))
            out_specs.append(VMEM)
        row, places = 0, {}
        for (stage, c), count in zip(group, counts):
            level = level_of(stage)
            plan = {
                "stage": stage,
                "rows": count,
                "ours": (operand(ours[c][0]), ours[c][1]),
                "theirs": (operand(theirs[c][0]), theirs[c][1]),
            }
            plan["weights"] = pair_of((weights if stage < LEVELS else flipped)[level])
            if stage == LEVELS - 1:
                plan["flipped"] = pair_of(flipped[level])
            if sends:
                plan["sent"] = (0, row)
            if LEVELS - 1 <= stage < 8:
                plan["kept"] = len(outs)
                outs.append(rows_of(count))
                out_specs.append(VMEM)
            if stage == LEVELS - 1:
                plan["observed"] = operand(observed)
            if stage in (LEVELS - 1, 8):
                if stage not in places:
                    if stage in results:
                        aliases[operand(results[stage], HBM)] = len(outs)
                    places[stage] = len(outs)
                    outs.append(pltpu.HBM((boxes, parts, rows, k), F32))
                    out_specs.append(HBM)
                plan["result"] = (places[stage], edges[c], len(scratch), len(scratch) + 1)
                scratch += [rows_of(count), pltpu.SemaphoreType.DMA((boxes,))]
            plans.append(plan)
            row += count
        operand(token, ANY)
        first, second = len(operands), len(operands) + len(outs)
        for plan in plans:
            if "sent" in plan:
                plan["sent"] = (first + plan["sent"][0], plan["sent"][1])
            if "kept" in plan:
                plan["kept"] += first
            if "result" in plan:
                whole, at, buffer, sems = plan["result"]
                plan["result"] = (first + whole, at, second + buffer, second + sems)
        tasks = tuple(Task(**plan) for plan in plans)
        made = call(functools.partial(group_kernel, tasks), operands, specs, outs, out_specs, scratch, aliases)
        token = made[0]
        for stage, at in places.items():
            results[stage] = made[at]
        if not sends:
            continue
        received = swap(token, sends)
        for task, (stage, c) in zip(tasks, group):
            at = task.sent[1]
            ours[c] = (token, at) if task.kept < 0 else (made[task.kept - first], 0)
            theirs[c] = (received, at)
    return results[LEVELS - 1], results[8]


def level_of(stage):
    return stage if stage < LEVELS else 2 * LEVELS - 2 - stage


def exchange_of(stage):
    return stage + 1 if stage < LEVELS - 1 else level_of(stage)


def solution(mesh):
    boxes = P(("wide", "narrow"), None, None, None)
    matrices = P(None, ("wide", "narrow"), None, None, None)

    return jax.shard_map(
        shards, mesh=mesh, in_specs=(boxes, boxes, matrices, matrices), out_specs=(boxes, boxes), check_vma=False
    )
```

```python
import functools
from typing import NamedTuple

import jax
import jax.numpy as jnp
from jax import lax
from jax.experimental import pallas as pl
from jax.experimental.pallas import tpu as pltpu
from jax.sharding import PartitionSpec as P


LEVELS = 5
BF, F32 = jnp.bfloat16, jnp.float32
SHARES = (3, 3, 3, 4, 3)
ORDER = (((9, 0),), ((0, 0),), ((1, 0),), ((9, 2),), ((0, 3),), ((0, 1),), ((0, 2),), ((1, 1),), ((9, 3),), ((10, 1),), ((0, 4),), ((2, 0),), ((1, 2),), ((2, 1),), ((3, 0),), ((9, 4),), ((3, 1),), ((4, 0),), ((1, 3),), ((2, 2),), ((4, 1),), ((1, 4),), ((3, 2),), ((5, 0),), ((2, 3),), ((5, 1),), ((4, 2),), ((6, 0),), ((2, 4),), ((3, 3),), ((6, 1),), ((5, 2),), ((4, 3),), ((3, 4),), ((6, 2),), ((5, 3),), ((7, 0),), ((4, 4),), ((6, 3),), ((10, 0),), ((5, 4),), ((7, 2),), ((7, 1),), ((8, 0),), ((6, 4),), ((8, 2),), ((8, 1),), ((7, 3),), ((8, 3),), ((7, 4),), ((8, 4),))
VMEM = pl.BlockSpec(memory_space=pltpu.VMEM)
HBM = pl.BlockSpec(memory_space=pltpu.HBM)
ANY = pl.BlockSpec(memory_space=pl.ANY)


def split(x):
    high = x.astype(BF)
    return high, (x - high.astype(F32)).astype(BF)


def dot(a, b):
    return lax.dot_general(a, b, (((1,), (0,)), ((), ())), preferred_element_type=F32)


def product(ur, ui, high, low, adjoint):
    rows = ur.shape[0]
    rh, rl = split(ur)
    ih, il = split(ui)
    both = jnp.concatenate([rh, rl, ih, il], 0)
    tops = jnp.concatenate([rh, ih], 0)

    def real(k):
        a, c = dot(both, high[k]), dot(tops, low[k])
        return a[:rows] + a[rows : 2 * rows] + c[:rows], a[2 * rows : 3 * rows] + a[3 * rows :] + c[rows:]

    rr, ir = real(0)
    ri, ii = real(1)
    return (rr + ii, ir - ri) if adjoint else (rr - ii, ri + ir)


def store_transposes(s, b, high, low, flipped):
    for k in range(high.shape[2]):
        flipped[0][s, b, k] = high[s, b, k].T
        flipped[1][s, b, k] = low[s, b, k].T


def prepare_kernel(levels, flips, own, partner, *refs):
    made, (buffer, sems) = refs[-2 - (4 if flips else 2) * len(levels) : -2], refs[-2:]
    boxes = made[0].shape[1]
    copies = [
        [
            (s, b, pltpu.make_async_copy(source.at[level, b], buffer.at[n, s, b], sems.at[n, s, b]))
            for s, source in enumerate((own, partner))
            for b in range(boxes)
        ]
        for n, level in enumerate(levels)
    ]
    for row in copies:
        for _, _, copy in row:
            copy.start()
    for n, row in enumerate(copies):
        high, low = made[2 * n : 2 * n + 2]
        for s, b, copy in row:
            copy.wait()
            high[s, b], low[s, b] = split(buffer[n, s, b])
            if flips:
                store_transposes(s, b, high, low, made[2:])


def flip_kernel(high, low, token, *flipped):
    for s in range(high.shape[0]):
        for b in range(high.shape[1]):
            store_transposes(s, b, high, low, flipped)


class Task(NamedTuple):
    stage: int
    rows: int
    ours: tuple
    theirs: tuple
    weights: int
    flipped: int = -1
    sent: tuple = ()
    kept: int = -1
    observed: int = -1
    result: tuple = ()


def group_kernel(tasks, flag, *refs):
    copies = []
    if flag >= 0:
        refs[flag][...] = jnp.zeros_like(refs[flag])
    for task in tasks:
        (ours, start), (theirs, other) = ((refs[ref], pl.ds(row, task.rows)) for ref, row in (task.ours, task.theirs))
        high, low = refs[task.weights], refs[task.weights + 1]
        boxes = range(ours.shape[0])
        if task.sent:
            out, at = refs[task.sent[0]], pl.ds(task.sent[1], task.rows)
        if task.result:
            whole, row, buffer, sems = task.result
            buffer, final = refs[buffer], pl.ds(row, task.rows)
            writes = [
                pltpu.make_async_copy(buffer.at[b], refs[whole].at[b, :, final], refs[sems].at[b]) for b in boxes
            ]
            copies += writes
        if task.stage < LEVELS:
            for b in boxes:
                p = b ^ 1 if task.stage == 0 else b
                r0, i0 = product(ours[b, 0, start], ours[b, 1, start], high.at[0, b], low.at[0, b], False)
                r1, i1 = product(theirs[p, 0, other], theirs[p, 1, other], high.at[1, b], low.at[1, b], False)
                if task.stage < LEVELS - 1:
                    out[b, 0, at], out[b, 1, at] = r0 + r1, i0 + i1
                else:
                    observed = refs[task.observed]
                    buffer[b, 0] = r0 + r1 - observed[b, 0, final]
                    buffer[b, 1] = i0 + i1 - observed[b, 1, final]
                    writes[b].start()
            if task.stage < LEVELS - 1:
                continue
            grads = [(buffer[b, 0], buffer[b, 1]) for b in boxes]
            high, low = refs[task.flipped], refs[task.flipped + 1]
        else:
            grads = [
                (ours[b, 0, start] + theirs[b, 0, other], ours[b, 1, start] + theirs[b, 1, other]) for b in boxes
            ]
        for b in boxes:
            if task.sent:
                out[b, 0, at], out[b, 1, at] = product(*grads[b], high.at[1, b], low.at[1, b], True)
            sr, si = product(*grads[b], high.at[0, b], low.at[0, b], True)
            if task.sent:
                kept = refs[task.kept]
                kept[b, 0], kept[b, 1] = sr, si
            else:
                p = b ^ 1
                tr, ti = product(*grads[p], high.at[1, p], low.at[1, p], True)
                buffer[b, 0], buffer[b, 1] = sr + tr, si + ti
                writes[b].start()
    for copy in copies:
        copy.wait()


def call(kernel, operands, specs, outs, out_specs, scratch=(), aliases=None):
    return pl.pallas_call(
        kernel,
        out_shape=outs,
        in_specs=specs,
        out_specs=out_specs,
        scratch_shapes=scratch,
        input_output_aliases=aliases or {},
        compiler_params=pltpu.CompilerParams(vmem_limit_bytes=10 << 20),
    )(*operands)


def shards(model, observed, own_weights, partner_weights):
    narrow, wide = lax.axis_size("narrow"), lax.axis_size("wide")
    exchanges = {1: ("narrow", 1), 2: ("narrow", narrow // 2), 3: ("wide", 1), 4: ("wide", wide // 2)}
    boxes, parts, rows, k = model.shape
    edges = [sum(SHARES[:c]) * rows // sum(SHARES) for c in range(len(SHARES) + 1)]

    def swap(value, level):
        axis, mask = exchanges[level]
        return lax.ppermute(value, axis, [(i, i ^ mask) for i in range(lax.axis_size(axis))])

    def rows_of(count):
        return pltpu.VMEM((boxes, parts, count, k), F32)

    model, observed = (pltpu.with_memory_space_constraint(x, pltpu.VMEM) for x in (model, observed))
    stored = [pltpu.with_memory_space_constraint(x, pltpu.HBM) for x in (own_weights, partner_weights)]
    matrices = (2,) + own_weights.shape[1:]
    weights, flipped = {}, {}
    later = {c for group in ORDER for stage, c in group if stage == 10}
    ours = {c: (model, edges[c]) for c in range(len(SHARES))}
    theirs = dict(ours)
    results = {}
    token = None

    for group in ORDER:
        stage, c = group[0]
        if stage == 9:
            tokens = [] if token is None else [token]
            levels = (0, 1) if c == 0 else (c,)
            flips = c not in later
            count = (4 if flips else 2) * len(levels)
            made = call(
                functools.partial(prepare_kernel, levels, flips),
                stored + tokens,
                [HBM, HBM] + [ANY] * len(tokens),
                (pltpu.VMEM(matrices, BF),) * count,
                (VMEM,) * count,
                [pltpu.VMEM((len(levels), *matrices), F32), pltpu.SemaphoreType.DMA((len(levels), 2, boxes))],
            )
            if flips:
                weights[c], flipped[c] = made[:2], made[2:]
            else:
                for n, level in enumerate(levels):
                    weights[level] = made[2 * n : 2 * n + 2]
            token = made[0]
            continue
        if stage == 10:
            flipped[c] = call(
                flip_kernel, [*weights[c], token], [VMEM, VMEM, ANY], (pltpu.VMEM(matrices, BF),) * 2, (VMEM,) * 2
            )
            token = flipped[c][0]
            continue
        operands, specs, outs, out_specs, scratch, aliases, plans = [], [], [], [], [], {}, []

        def operand(array, spec=VMEM):
            for at, known in enumerate(operands):
                if known is array:
                    return at
            operands.append(array)
            specs.append(spec)
            return len(operands) - 1

        def pair_of(matrices):
            at = operand(matrices[0])
            operand(matrices[1])
            return at

        counts = [edges[c + 1] - edges[c] for _, c in group]
        sends = exchange_of(stage)
        if sends:
            outs.append(rows_of(sum(counts)))
            out_specs.append(VMEM)
        else:
            outs.append(pltpu.VMEM((8, 128), F32))
            out_specs.append(VMEM)
        row, places = 0, {}
        for (stage, c), count in zip(group, counts):
            level = level_of(stage)
            plan = {
                "stage": stage,
                "rows": count,
                "ours": (operand(ours[c][0]), ours[c][1]),
                "theirs": (operand(theirs[c][0]), theirs[c][1]),
            }
            plan["weights"] = pair_of((weights if stage < LEVELS else flipped)[level])
            if stage == LEVELS - 1:
                plan["flipped"] = pair_of(flipped[level])
            if sends:
                plan["sent"] = (0, row)
            if LEVELS - 1 <= stage < 8:
                plan["kept"] = len(outs)
                outs.append(rows_of(count))
                out_specs.append(VMEM)
            if stage == LEVELS - 1:
                plan["observed"] = operand(observed)
            if stage in (LEVELS - 1, 8):
                if stage not in places:
                    if stage in results:
                        aliases[operand(results[stage], HBM)] = len(outs)
                    places[stage] = len(outs)
                    outs.append(pltpu.HBM((boxes, parts, rows, k), F32))
                    out_specs.append(HBM)
                plan["result"] = (places[stage], edges[c], len(scratch), len(scratch) + 1)
                scratch += [rows_of(count), pltpu.SemaphoreType.DMA((boxes,))]
            plans.append(plan)
            row += count
        operand(token, ANY)
        first, second = len(operands), len(operands) + len(outs)
        for plan in plans:
            if "sent" in plan:
                plan["sent"] = (first + plan["sent"][0], plan["sent"][1])
            if "kept" in plan:
                plan["kept"] += first
            if "result" in plan:
                whole, at, buffer, sems = plan["result"]
                plan["result"] = (first + whole, at, second + buffer, second + sems)
        tasks = tuple(Task(**plan) for plan in plans)
        flag = -1 if sends else first
        made = call(functools.partial(group_kernel, tasks, flag), operands, specs, outs, out_specs, scratch, aliases)
        token = made[0]
        for stage, at in places.items():
            results[stage] = made[at]
        if not sends:
            continue
        received = swap(token, sends)
        for task, (stage, c) in zip(tasks, group):
            at = task.sent[1]
            ours[c] = (token, at) if task.kept < 0 else (made[task.kept - first], 0)
            theirs[c] = (received, at)
    return results[LEVELS - 1], results[8]


def level_of(stage):
    return stage if stage < LEVELS else 2 * LEVELS - 2 - stage


def exchange_of(stage):
    return stage + 1 if stage < LEVELS - 1 else level_of(stage)


def solution(mesh):
    boxes = P(("wide", "narrow"), None, None, None)
    matrices = P(None, ("wide", "narrow"), None, None, None)

    return jax.shard_map(
        shards, mesh=mesh, in_specs=(boxes, boxes, matrices, matrices), out_specs=(boxes, boxes), check_vma=False
    )
```
